32 devices in a mesh: grp: 2 (over y), blk: 4 (over z), head: 2 (over x), sub: 2 (over core).
Axes of the slice: x: 2, y: 2, z: 4, core: 2. Of those that a mesh axis runs over, the one named last changes fastest.
Arguments:
- queries: bfloat16 [4096, 4096], P(('grp', 'blk', 'head', 'sub')), parts along dimension 0, may hold values from -46 to 46
- keys: bfloat16 [4096, 4096], P(('grp', 'blk', 'head', 'sub')), parts along dimension 0, may hold values from -4 to 4
- values: bfloat16 [4096, 4096], P(('grp', 'blk', 'head', 'sub')), parts along dimension 0, may hold values from -6 to 6
- block_lists: int32 [32, 16, 8], replicated, may hold values from 0 to 15, as said below
Outputs:
- attended: bfloat16 [4096, 4096], P(('grp', 'blk', 'head', 'sub')), parts along dimension 0
The draws below stay inside these ranges and needn't reach their ends.
There are 2 independent parts, one for each index of `grp`. The reference program is written for one: setup_inputs(seed, part) draws one part's arguments, and reference() takes and returns one part's arrays. A program takes and returns all parts, laid end to end along the dimension named above; an argument that names none is the same for every part. Nothing has to cross between parts.
Inputs may be any that keep to these rules, and one draw needn't show every extreme that they name: `block_lists`: the first entry of every list is the query tile itself; entries may repeat. Tiles are numbered frame by frame, 4 to a frame. In each head either all entries lie in the query tile's frame or the frames next to it, or all entries have the query tile's position within its frame.
All inputs are finite; a program needn't handle non-finite values.
Results may differ from the reference program's by a relative error of at most 0.0065.
Values may be sent and summed in bfloat16 or wider, within the bound.
A program may use at most 64 MiB of HBM per device.

```python
import math
import jax
import jax.numpy as jnp
from jax import lax

HEADS = 32
HEAD_DIM = 128
TILE = 128
LIST = 8
FRAME_TILES = 4
SEQ = 2048
QTILES = 16


def draw_pair(key):
    col_count = HEADS * HEAD_DIM
    seed_query, seed_keys = jax.random.split(jax.random.fold_in(key, 11), 2)
    query_draw = jnp.clip(jax.random.normal(seed_query, (SEQ, col_count), jnp.float32), -4.0, 4.0)
    keys_draw = jnp.clip(jax.random.normal(seed_keys, (SEQ, col_count), jnp.float32), -4.0, 4.0)
    return (query_draw, keys_draw)


def draw_queries(key, part):
    query_draw, keys_draw = draw_pair(key)
    return query_draw.astype(jnp.bfloat16)


def draw_keys(key, part):
    query_draw, keys_draw = draw_pair(key)
    return keys_draw.astype(jnp.bfloat16)


def draw_block_lists(key, part):
    seed_one, seed_two, seed_three, seed_four = jax.random.split(jax.random.fold_in(key, 23), 4)
    frame_count = QTILES // FRAME_TILES
    shape_all = (HEADS, QTILES, LIST)
    pattern = jax.random.randint(seed_one, (HEADS, 1, 1), 0, 2)
    tile_index = jnp.arange(QTILES, dtype=jnp.int32)[None, :, None]
    frame_no = tile_index // FRAME_TILES
    slot_no = tile_index % FRAME_TILES
    frame_step = jax.random.randint(seed_two, shape_all, -1, 2)
    near_frame = jnp.clip(frame_no + frame_step, 0, frame_count - 1)
    near_slot = jax.random.randint(seed_three, shape_all, 0, FRAME_TILES)
    spatial_tile = near_frame * FRAME_TILES + near_slot
    far_frame = jax.random.randint(seed_four, shape_all, 0, frame_count)
    temporal_tile = far_frame * FRAME_TILES + slot_no
    chosen = jnp.where(pattern == 1, temporal_tile, spatial_tile)
    first_col = jnp.arange(LIST, dtype=jnp.int32)[None, None, :] == 0
    return jnp.where(first_col, tile_index, chosen).astype(jnp.int32)


def block_levels(stream_key, dims, shards, low, largest):
    factor_of = 1.0
    for position, shards_of in shards:
        heights = jax.random.uniform(jax.random.fold_in(jax.random.fold_in(stream_key, 6), position), (shards_of,), jnp.float32, low / len(shards), largest / len(shards))
        factor_of = factor_of * jnp.repeat(jnp.exp(heights), dims[position] // shards_of).reshape((-1,) + (1,) * (len(dims) - 1 - position))
    return factor_of


def gaussian(stream_key, extent, width, reach, cuts=(), kind=jnp.bfloat16):
    gain = block_levels(stream_key, extent, cuts, -0.22, 0.18) if cuts else 1.0
    result = jax.random.normal(stream_key, extent, jnp.float32) * width * gain
    return jnp.minimum(jnp.maximum(result, -reach), reach).astype(kind)


def setup_inputs(seed: int = 0, part: int = 0) -> dict:
    splits = jax.random.split(jax.random.key(seed), 5)
    part_splits = jax.random.split(jax.random.fold_in(splits[4], part), 5)
    return {
        "queries": draw_queries(jax.random.fold_in(jax.random.fold_in(splits[4], part), 71), part),
        "keys": draw_keys(jax.random.fold_in(jax.random.fold_in(splits[4], part), 71), part),
        "values": gaussian(part_splits[2], (SEQ, HEADS * HEAD_DIM), 1.0, 6.0, ((0, 16),)),
        "block_lists": draw_block_lists(jax.random.fold_in(splits[4], 71), part),
    }


def reference(queries, keys, values, block_lists):
    tile_ids = jnp.arange(QTILES, dtype=jnp.int32)
    tile_mask = jnp.any(block_lists[:, :, :, None] == tile_ids, axis=2)
    score_scale = 1.0 / math.sqrt(HEAD_DIM)

    def one_head(head_no):
        col_start = (head_no * HEAD_DIM).astype(jnp.int32)
        q_head = lax.dynamic_slice_in_dim(queries, col_start, HEAD_DIM, 1)
        k_head = lax.dynamic_slice_in_dim(keys, col_start, HEAD_DIM, 1)
        v_head = lax.dynamic_slice_in_dim(values, col_start, HEAD_DIM, 1)
        allowed = jnp.repeat(jnp.repeat(tile_mask[head_no], TILE, axis=0), TILE, axis=1)
        scores = jnp.dot(q_head, k_head.T, preferred_element_type=jnp.float32) * score_scale
        row_top = lax.optimization_barrier(jnp.max(jnp.where(allowed, scores, -jnp.inf), axis=1, keepdims=True))
        weights = jnp.where(allowed, jnp.exp(scores - row_top), 0.0)
        row_total = lax.optimization_barrier(jnp.sum(weights, axis=1, keepdims=True))
        numerator = jnp.dot(weights.astype(jnp.bfloat16), v_head, preferred_element_type=jnp.float32)
        return (numerator / row_total).astype(jnp.bfloat16)
    heads_out = lax.map(one_head, jnp.arange(HEADS, dtype=jnp.int32))
    return jnp.transpose(heads_out, (1, 0, 2)).reshape(SEQ, HEADS * HEAD_DIM)
```

```python
import functools
import math

import jax
import jax.numpy as jnp
from jax import lax
from jax.experimental import pallas as pl
from jax.experimental.pallas import tpu as pltpu
from jax.sharding import PartitionSpec as P

HEADS = 32
HEAD_DIM = 128
TILE = 128


NEG_FLOOR = -1e30


def query_rows(block_lists, first_head, heads_here, query_tokens):
    tile_ids = jnp.arange(block_lists.shape[1], dtype=jnp.int32)
    lists_local = lax.dynamic_slice_in_dim(block_lists, first_head, heads_here, 0)
    tile_mask = jnp.any(lists_local[:, :, :, None] == tile_ids, axis=2).astype(jnp.bfloat16)
    query_onehot = ((query_tokens // TILE)[:, None] == tile_ids[None, :]).astype(jnp.bfloat16)
    listed = jnp.einsum("qi,hij->hqj", query_onehot, tile_mask, preferred_element_type=jnp.float32)
    return listed.astype(jnp.bfloat16)


def attend_block(state_now, key_block, value_block, allowed, query_local, score_scale):
    top_old, total_old, accum_old = state_now
    scores = (
        jnp.einsum("qhd,khd->hqk", query_local, key_block, preferred_element_type=jnp.float32)
        * score_scale
    )
    top_new = jnp.maximum(top_old, jnp.max(jnp.where(allowed, scores, NEG_FLOOR), axis=2))
    factor = jnp.exp(top_old - top_new)
    weights = jnp.where(allowed, jnp.exp(scores - top_new[:, :, None]), 0.0)
    total_new = total_old * factor + jnp.sum(weights, axis=2)
    product = jnp.einsum(
        "hqk,khd->qhd",
        weights.astype(jnp.bfloat16),
        value_block,
        preferred_element_type=jnp.float32,
    )
    accum_new = accum_old * jnp.transpose(factor)[:, :, None] + product
    return (top_new, total_new, accum_new)


def make_step(query_local, listed_rows, key_token, block_len, tile_total):
    score_scale = 1.0 / math.sqrt(HEAD_DIM)
    tile_ids = jnp.arange(tile_total, dtype=jnp.int32)

    def fold_step(state_now, piece, first_row):
        key_piece, value_piece = piece
        block_count = key_piece.shape[0] // block_len

        def one_block(block_index, state_in):
            key_block = lax.dynamic_slice_in_dim(key_piece, block_index * block_len, block_len, 0)
            value_block = lax.dynamic_slice_in_dim(
                value_piece, block_index * block_len, block_len, 0
            )
            positions = block_index * block_len + jnp.arange(block_len, dtype=jnp.int32)
            key_tiles = key_token(positions) // TILE
            key_onehot = (tile_ids[:, None] == key_tiles[None, :]).astype(jnp.bfloat16)
            allowed = (
                jnp.einsum(
                    "hqj,jk->hqk", listed_rows, key_onehot, preferred_element_type=jnp.float32
                )
                > 0.5
            )
            result = attend_block(
                state_in, key_block, value_block, allowed, query_local, score_scale
            )
            return result

        return lax.fori_loop(0, block_count, one_block, state_now)

    return fold_step


def start_state(heads_here, block_len):
    top_all = jnp.full((heads_here, block_len), NEG_FLOOR, jnp.float32)
    total_all = jnp.zeros((heads_here, block_len), jnp.float32)
    accum_all = jnp.zeros((block_len, heads_here, HEAD_DIM), jnp.float32)
    return (top_all, total_all, accum_all)


def normalize(state_end):
    top_all, total_all, accum_all = state_end
    return (accum_all / jnp.transpose(total_all)[:, :, None]).astype(jnp.bfloat16)


def per_device(queries, keys, values, block_lists):
    row_count, col_count = queries.shape
    n_head = lax.axis_size("head")
    n_sub = lax.axis_size("sub")
    blk_index = lax.axis_index("blk")
    head_index = lax.axis_index("head")
    sub_index = lax.axis_index("sub")
    tile_total = block_lists.shape[1]
    heads_here = HEADS // (n_head * n_sub)
    block_len = row_count * n_head * n_sub

    def inward(tensor):
        return tensor.reshape(1, 1, row_count, n_head, n_sub, heads_here * HEAD_DIM)

    query_six, keys_six, values_six = (
        lax.all_to_all(
            lax.all_to_all(inward(queries), "head", split_axis=3, concat_axis=1, tiled=True),
            "sub",
            split_axis=4,
            concat_axis=0,
            tiled=True,
        ),
        lax.all_to_all(
            lax.all_to_all(inward(keys), "head", split_axis=3, concat_axis=1, tiled=True),
            "sub",
            split_axis=4,
            concat_axis=0,
            tiled=True,
        ),
        lax.all_to_all(
            lax.all_to_all(inward(values), "head", split_axis=3, concat_axis=1, tiled=True),
            "sub",
            split_axis=4,
            concat_axis=0,
            tiled=True,
        ),
    )
    query_local = query_six.reshape(block_len, heads_here, HEAD_DIM)
    keys_local = keys_six.reshape(block_len, heads_here, HEAD_DIM)
    values_local = values_six.reshape(block_len, heads_here, HEAD_DIM)

    def key_token(positions):
        source_dev = positions // block_len
        within = positions % block_len
        sub_source = within // (n_head * row_count)
        head_source = within // row_count % n_head
        offset = within % row_count
        return ((source_dev * n_head + head_source) * n_sub + sub_source) * row_count + offset

    query_tokens = key_token(blk_index * block_len + jnp.arange(block_len, dtype=jnp.int32))
    first_head = (head_index * n_sub + sub_index) * heads_here
    listed_rows = query_rows(block_lists, first_head, heads_here, query_tokens)
    fold_step = make_step(query_local, listed_rows, key_token, block_len, tile_total)
    state_end = fold_step(
        start_state(heads_here, block_len),
        (
            lax.all_gather(keys_local, "blk", axis=0, tiled=True),
            lax.all_gather(values_local, "blk", axis=0, tiled=True),
        ),
        jnp.int32(0),
    )
    result_rows = normalize(state_end)
    attended = result_rows.reshape(n_sub, n_head, row_count, 1, 1, heads_here * HEAD_DIM)
    returned = lax.all_to_all(
        lax.all_to_all(attended, "head", split_axis=1, concat_axis=3, tiled=True),
        "sub",
        split_axis=0,
        concat_axis=4,
        tiled=True,
    )
    return returned.reshape(row_count, col_count)


def attend_tile(lists, buf, tile_out, h, i):
    score_scale = 1.0 / math.sqrt(HEAD_DIM)
    entries = lists.shape[2]
    query = buf[0, i]
    ids = [lists[h, i, e] for e in range(entries)]
    scores, top = [], None
    for e in range(entries):
        s = lax.dot_general(
            query, buf[1, ids[e]], (((1,), (1,)), ((), ())), preferred_element_type=jnp.float32
        ) * score_scale
        scores.append(s)
        top = s if top is None else jnp.maximum(top, s)
    row_top = jnp.max(top, axis=1, keepdims=True)
    total, accum = None, None
    for e in range(entries):
        w = jnp.exp(scores[e] - row_top)
        if e:
            repeat = ids[e] == ids[0]
            for f in range(1, e):
                repeat = jnp.logical_or(repeat, ids[e] == ids[f])
            w = w * jnp.where(repeat, 0.0, 1.0)
        part = jnp.dot(
            w.astype(jnp.bfloat16), buf[2, ids[e]], preferred_element_type=jnp.float32
        )
        total = w if total is None else total + w
        accum = part if accum is None else accum + part
    row_total = jnp.sum(total, axis=1, keepdims=True)
    tile_out[h, i] = (accum / row_total).astype(jnp.bfloat16)


def exchange_kernel(sizes, heads_here, q_ref, k_ref, v_ref, lists_ref, out_ref, tile_out,
                    lists, send_sem, recv_sem, local_sem, list_sem, *bufs):
    n_blk, n_head, n_sub = sizes
    count = n_blk * n_head * n_sub
    me = (lax.axis_index("blk") * n_head + lax.axis_index("head")) * n_sub + lax.axis_index("sub")
    sources = (q_ref, k_ref, v_ref)

    def coords(rank):
        return {
            "blk": rank // (n_head * n_sub),
            "head": rank // n_sub % n_head,
            "sub": rank % n_sub,
        }

    def peer(d):
        return (me + d) % count

    def columns(rank, h):
        return pl.ds(pl.multiple_of((rank * heads_here + h) * HEAD_DIM, HEAD_DIM), HEAD_DIM)

    def inward(t, h, target, sender):
        return pltpu.make_async_remote_copy(
            src_ref=sources[t].at[:, columns(target, h)],
            dst_ref=bufs[h].at[t, sender],
            send_sem=send_sem.at[t, h, target],
            recv_sem=recv_sem.at[t, h, sender],
            device_id=coords(target),
            device_id_type=pl.DeviceIdType.MESH,
        )

    def outward(h, target, sender):
        return pltpu.make_async_remote_copy(
            src_ref=tile_out.at[h, target],
            dst_ref=out_ref.at[:, columns(sender, h)],
            send_sem=send_sem.at[3, h, target],
            recv_sem=recv_sem.at[3, h, sender],
            device_id=coords(target),
            device_id_type=pl.DeviceIdType.MESH,
        )

    def own_in(t, h):
        return pltpu.make_async_copy(
            sources[t].at[:, columns(me, h)], bufs[h].at[t, me], local_sem.at[t, h]
        )

    def own_out(h):
        return pltpu.make_async_copy(
            tile_out.at[h, me], out_ref.at[:, columns(me, h)], local_sem.at[3, h]
        )

    own_lists = pltpu.make_async_copy(
        lists_ref.at[pl.ds(me * heads_here, heads_here)], lists, list_sem
    )
    own_lists.start()
    for h in range(heads_here):
        for t in range(3):
            own_in(t, h).start()

    barrier = pltpu.get_barrier_semaphore()

    def greet(d, carry):
        pl.semaphore_signal(
            barrier, inc=1, device_id=coords(peer(d)), device_id_type=pl.DeviceIdType.MESH
        )
        return carry

    lax.fori_loop(1, count, greet, 0)
    pl.semaphore_wait(barrier, count - 1)

    for h in range(heads_here):
        def send_in(d, carry, h=h):
            for t in range(3):
                inward(t, h, peer(d), me).start()
            return carry

        lax.fori_loop(1, count, send_in, 0)

    own_lists.wait()
    for h in range(heads_here):
        for t in range(3):
            own_in(t, h).wait()

        def arrive(d, carry, h=h):
            for t in range(3):
                inward(t, h, me, peer(d)).wait_recv()
            return carry

        lax.fori_loop(1, count, arrive, 0)

        def work(d, carry, h=h):
            attend_tile(lists, bufs[h], tile_out, h, peer(d))

            @pl.when(d > 1)
            def _():
                outward(h, peer(d - 1), me).start()

            return carry

        lax.fori_loop(1, count, work, 0)
        attend_tile(lists, bufs[h], tile_out, h, me)
        outward(h, peer(count - 1), me).start()
        own_out(h).start()

    for h in range(heads_here):
        own_out(h).wait()

        def finish(d, carry, h=h):
            other = peer(d)
            for t in range(3):
                inward(t, h, other, me).wait_send()
            outward(h, other, me).wait_send()
            outward(h, me, other).wait_recv()
            return carry

        lax.fori_loop(1, count, finish, 0)


def whole_exchange(sizes, queries, keys, values, block_lists):
    count = sizes[0] * sizes[1] * sizes[2]
    heads_here = HEADS // count
    rows = queries.shape[0]
    tiles, entries = block_lists.shape[1:]
    any_space = pl.BlockSpec(memory_space=pl.ANY)
    return pl.pallas_call(
        functools.partial(exchange_kernel, sizes, heads_here),
        out_shape=jax.ShapeDtypeStruct(queries.shape, jnp.bfloat16),
        in_specs=[any_space] * 4,
        out_specs=any_space,
        scratch_shapes=[
            pltpu.VMEM((heads_here, count, rows, HEAD_DIM), jnp.bfloat16),
            pltpu.SMEM((heads_here, tiles, entries), jnp.int32),
            pltpu.SemaphoreType.DMA((4, heads_here, count)),
            pltpu.SemaphoreType.DMA((4, heads_here, count)),
            pltpu.SemaphoreType.DMA((4, heads_here)),
            pltpu.SemaphoreType.DMA,
            *[pltpu.VMEM((3, count, rows, HEAD_DIM), jnp.bfloat16) for _ in range(heads_here)],
        ],
        compiler_params=pltpu.CompilerParams(collective_id=0, has_side_effects=True),
    )(queries, keys, values, block_lists)


def solution(mesh):
    sizes = tuple(mesh.shape[axis] for axis in ("blk", "head", "sub"))
    count = sizes[0] * sizes[1] * sizes[2]

    def body(queries, keys, values, block_lists):
        if queries.shape[0] == TILE and HEADS % count == 0:
            return whole_exchange(sizes, queries, keys, values, block_lists)
        return per_device(queries, keys, values, block_lists)

    in_specs = (
        P(("grp", "blk", "head", "sub"), None),
        P(("grp", "blk", "head", "sub"), None),
        P(("grp", "blk", "head", "sub"), None),
        P(),
    )
    out_specs = P(("grp", "blk", "head", "sub"), None)
    return jax.shard_map(
        body, mesh=mesh, in_specs=in_specs, out_specs=out_specs, check_vma=False
    )
```

```python
import functools
import math

import jax
import jax.numpy as jnp
from jax import lax
from jax.experimental import pallas as pl
from jax.experimental.pallas import tpu as pltpu
from jax.sharding import PartitionSpec as P

HEADS = 32
HEAD_DIM = 128
TILE = 128


NEG_FLOOR = -1e30


def query_rows(block_lists, first_head, heads_here, query_tokens):
    tile_ids = jnp.arange(block_lists.shape[1], dtype=jnp.int32)
    lists_local = lax.dynamic_slice_in_dim(block_lists, first_head, heads_here, 0)
    tile_mask = jnp.any(lists_local[:, :, :, None] == tile_ids, axis=2).astype(jnp.bfloat16)
    query_onehot = ((query_tokens // TILE)[:, None] == tile_ids[None, :]).astype(jnp.bfloat16)
    listed = jnp.einsum("qi,hij->hqj", query_onehot, tile_mask, preferred_element_type=jnp.float32)
    return listed.astype(jnp.bfloat16)


def attend_block(state_now, key_block, value_block, allowed, query_local, score_scale):
    top_old, total_old, accum_old = state_now
    scores = (
        jnp.einsum("qhd,khd->hqk", query_local, key_block, preferred_element_type=jnp.float32)
        * score_scale
    )
    top_new = jnp.maximum(top_old, jnp.max(jnp.where(allowed, scores, NEG_FLOOR), axis=2))
    factor = jnp.exp(top_old - top_new)
    weights = jnp.where(allowed, jnp.exp(scores - top_new[:, :, None]), 0.0)
    total_new = total_old * factor + jnp.sum(weights, axis=2)
    product = jnp.einsum(
        "hqk,khd->qhd",
        weights.astype(jnp.bfloat16),
        value_block,
        preferred_element_type=jnp.float32,
    )
    accum_new = accum_old * jnp.transpose(factor)[:, :, None] + product
    return (top_new, total_new, accum_new)


def make_step(query_local, listed_rows, key_token, block_len, tile_total):
    score_scale = 1.0 / math.sqrt(HEAD_DIM)
    tile_ids = jnp.arange(tile_total, dtype=jnp.int32)

    def fold_step(state_now, piece, first_row):
        key_piece, value_piece = piece
        block_count = key_piece.shape[0] // block_len

        def one_block(block_index, state_in):
            key_block = lax.dynamic_slice_in_dim(key_piece, block_index * block_len, block_len, 0)
            value_block = lax.dynamic_slice_in_dim(
                value_piece, block_index * block_len, block_len, 0
            )
            positions = block_index * block_len + jnp.arange(block_len, dtype=jnp.int32)
            key_tiles = key_token(positions) // TILE
            key_onehot = (tile_ids[:, None] == key_tiles[None, :]).astype(jnp.bfloat16)
            allowed = (
                jnp.einsum(
                    "hqj,jk->hqk", listed_rows, key_onehot, preferred_element_type=jnp.float32
                )
                > 0.5
            )
            result = attend_block(
                state_in, key_block, value_block, allowed, query_local, score_scale
            )
            return result

        return lax.fori_loop(0, block_count, one_block, state_now)

    return fold_step


def start_state(heads_here, block_len):
    top_all = jnp.full((heads_here, block_len), NEG_FLOOR, jnp.float32)
    total_all = jnp.zeros((heads_here, block_len), jnp.float32)
    accum_all = jnp.zeros((block_len, heads_here, HEAD_DIM), jnp.float32)
    return (top_all, total_all, accum_all)


def normalize(state_end):
    top_all, total_all, accum_all = state_end
    return (accum_all / jnp.transpose(total_all)[:, :, None]).astype(jnp.bfloat16)


def per_device(queries, keys, values, block_lists):
    row_count, col_count = queries.shape
    n_head = lax.axis_size("head")
    n_sub = lax.axis_size("sub")
    blk_index = lax.axis_index("blk")
    head_index = lax.axis_index("head")
    sub_index = lax.axis_index("sub")
    tile_total = block_lists.shape[1]
    heads_here = HEADS // (n_head * n_sub)
    block_len = row_count * n_head * n_sub

    def inward(tensor):
        return tensor.reshape(1, 1, row_count, n_head, n_sub, heads_here * HEAD_DIM)

    query_six, keys_six, values_six = (
        lax.all_to_all(
            lax.all_to_all(inward(queries), "head", split_axis=3, concat_axis=1, tiled=True),
            "sub",
            split_axis=4,
            concat_axis=0,
            tiled=True,
        ),
        lax.all_to_all(
            lax.all_to_all(inward(keys), "head", split_axis=3, concat_axis=1, tiled=True),
            "sub",
            split_axis=4,
            concat_axis=0,
            tiled=True,
        ),
        lax.all_to_all(
            lax.all_to_all(inward(values), "head", split_axis=3, concat_axis=1, tiled=True),
            "sub",
            split_axis=4,
            concat_axis=0,
            tiled=True,
        ),
    )
    query_local = query_six.reshape(block_len, heads_here, HEAD_DIM)
    keys_local = keys_six.reshape(block_len, heads_here, HEAD_DIM)
    values_local = values_six.reshape(block_len, heads_here, HEAD_DIM)

    def key_token(positions):
        source_dev = positions // block_len
        within = positions % block_len
        sub_source = within // (n_head * row_count)
        head_source = within // row_count % n_head
        offset = within % row_count
        return ((source_dev * n_head + head_source) * n_sub + sub_source) * row_count + offset

    query_tokens = key_token(blk_index * block_len + jnp.arange(block_len, dtype=jnp.int32))
    first_head = (head_index * n_sub + sub_index) * heads_here
    listed_rows = query_rows(block_lists, first_head, heads_here, query_tokens)
    fold_step = make_step(query_local, listed_rows, key_token, block_len, tile_total)
    state_end = fold_step(
        start_state(heads_here, block_len),
        (
            lax.all_gather(keys_local, "blk", axis=0, tiled=True),
            lax.all_gather(values_local, "blk", axis=0, tiled=True),
        ),
        jnp.int32(0),
    )
    result_rows = normalize(state_end)
    attended = result_rows.reshape(n_sub, n_head, row_count, 1, 1, heads_here * HEAD_DIM)
    returned = lax.all_to_all(
        lax.all_to_all(attended, "head", split_axis=1, concat_axis=3, tiled=True),
        "sub",
        split_axis=0,
        concat_axis=4,
        tiled=True,
    )
    return returned.reshape(row_count, col_count)


NEAR_COUNTS = (0, 8, 12, 16, 20)


def attend_tile(ids, query, buf, first):
    score_scale = 1.0 / math.sqrt(HEAD_DIM)
    scores, top = [], None
    for tile in ids:
        s = lax.dot_general(
            query, buf[first, tile], (((1,), (1,)), ((), ())), preferred_element_type=jnp.float32
        ) * score_scale
        scores.append(s)
        top = s if top is None else jnp.maximum(top, s)
    row_top = jnp.max(top, axis=1, keepdims=True)
    total, accum = None, None
    for e, tile in enumerate(ids):
        w = jnp.exp(scores[e] - row_top)
        if e:
            repeat = tile == ids[0]
            for f in range(1, e):
                repeat = jnp.logical_or(repeat, tile == ids[f])
            w = w * jnp.where(repeat, 0.0, 1.0)
        part = jnp.dot(
            w.astype(jnp.bfloat16), buf[first + 1, tile], preferred_element_type=jnp.float32
        )
        total = w if total is None else total + w
        accum = part if accum is None else accum + part
    row_total = jnp.sum(total, axis=1, keepdims=True)
    return (accum / row_total).astype(jnp.bfloat16)


def exchange_kernel(sizes, near, stage, list_rows, landed, lists, list_sem, *scratch):
    n_blk, n_head, n_sub = sizes
    line_count = n_head * n_sub
    count = n_blk * line_count
    entries = lists.shape[2]
    near_here = near // line_count
    far = HEADS - near
    far_here = -(-far // count)
    far_in = scratch[:far_here]
    far_out = scratch[far_here : 2 * far_here]
    scratch = scratch[2 * far_here :]
    near_query = scratch[:near_here]
    near_kv = scratch[near_here : 2 * near_here]
    near_out = scratch[2 * near_here : 3 * near_here]
    far_send, far_recv, far_local = scratch[3 * near_here : 3 * near_here + 3]
    if near:
        near_send, near_recv, near_local, hop_send, hop_recv = scratch[3 * near_here + 3 :]

    blk = lax.axis_index("blk")
    line = lax.axis_index("head") * n_sub + lax.axis_index("sub")
    me = blk * line_count + line

    def remote(src, dst, send, recv, rank):
        return pltpu.make_async_remote_copy(
            src_ref=src,
            dst_ref=dst,
            send_sem=send,
            recv_sem=recv,
            device_id={
                "blk": rank // line_count,
                "head": rank // n_sub % n_head,
                "sub": rank % n_sub,
            },
            device_id_type=pl.DeviceIdType.MESH,
        )

    def peer(d):
        return (me + d) % count

    def line_peer(d):
        return (line + d) % line_count

    def far_number(rank, a):
        return a * count + rank // line_count + n_blk * (rank % line_count)

    def far_inward(t, a, target, sender):
        return remote(
            stage.at[t, near + far_number(target, a)], far_in[a].at[t, sender],
            far_send.at[t, a, target], far_recv.at[t, a, sender], target,
        )

    def far_outward(a, target, sender):
        return remote(
            far_out[a].at[target], landed.at[near + far_number(sender, a)],
            far_send.at[3, a, target], far_recv.at[3, a, sender], target,
        )

    def far_own_in(t, a):
        return pltpu.make_async_copy(
            stage.at[t, near + far_number(me, a)], far_in[a].at[t, me], far_local.at[t, a]
        )

    def far_own_out(a):
        return pltpu.make_async_copy(
            far_out[a].at[me], landed.at[near + far_number(me, a)], far_local.at[3, a]
        )

    def if_far(rank, a, action):
        if (a + 1) * count <= far:
            action()
        else:
            pl.when(far_number(rank, a) < far)(action)

    def near_slot(t, a, sender):
        if t == 0:
            return near_query[a].at[sender]
        return near_kv[a].at[t - 1, line_count + sender]

    def near_inward(t, a, target, sender):
        return remote(
            stage.at[t, a * line_count + target], near_slot(t, a, sender),
            near_send.at[t, a, target], near_recv.at[t, a, sender], blk * line_count + target,
        )

    def near_outward(a, target, sender):
        return remote(
            near_out[a].at[target], landed.at[a * line_count + sender],
            near_send.at[3, a, target], near_recv.at[3, a, sender], blk * line_count + target,
        )

    def near_own_in(t, a):
        return pltpu.make_async_copy(
            stage.at[t, a * line_count + line], near_slot(t, a, line), near_local.at[t, a]
        )

    def near_own_out(a):
        return pltpu.make_async_copy(
            near_out[a].at[line], landed.at[a * line_count + line], near_local.at[3, a]
        )

    def hop(a, direction):
        return remote(
            near_kv[a].at[:, pl.ds(line_count, line_count)],
            near_kv[a].at[:, pl.ds(2 * line_count * direction, line_count)],
            hop_send.at[a, direction], hop_recv.at[a, direction],
            (me + line_count if direction == 0 else me + count - line_count) % count,
        )

    def each_hop(action, sending):
        up, down = blk < n_blk - 1, blk > 0
        pl.when(up if sending else down)(functools.partial(action, 0))
        pl.when(down if sending else up)(functools.partial(action, 1))

    barrier = pltpu.get_barrier_semaphore()

    def greet(d, carry):
        rank = peer(d)
        pl.semaphore_signal(
            barrier, inc=1,
            device_id={
                "blk": rank // line_count,
                "head": rank // n_sub % n_head,
                "sub": rank % n_sub,
            },
            device_id_type=pl.DeviceIdType.MESH,
        )
        return carry

    lax.fori_loop(1, count, greet, 0)

    def own_list(a, far_head):
        slot = near + far_number(me, a) if far_head else a * line_count + line
        row = near_here + a if far_head else a
        return pltpu.make_async_copy(list_rows.at[slot], lists.at[row], list_sem.at[row])

    for a in range(near_here):
        own_list(a, False).start()
    for a in range(far_here):
        if_far(me, a, lambda a=a: own_list(a, True).start())
    pl.semaphore_wait(barrier, count - 1)

    for a in range(near_here):
        def near_send_in(d, carry, a=a):
            for t in (1, 2, 0):
                near_inward(t, a, line_peer(d), line).start()
            return carry

        lax.fori_loop(1, line_count, near_send_in, 0)
        for t in range(3):
            near_own_in(t, a).start()

    for a in range(far_here):
        def far_send_in(d, carry, a=a):
            def send(d=d):
                for t in range(3):
                    far_inward(t, a, peer(d), me).start()

            if_far(peer(d), a, send)
            return carry

        lax.fori_loop(1, count, far_send_in, 0)

        def own(a=a):
            for t in range(3):
                far_own_in(t, a).start()

        if_far(me, a, own)

    for a in range(near_here):
        for t in range(3):
            near_own_in(t, a).wait()

        def near_arrive(d, carry, a=a):
            for t in range(3):
                near_inward(t, a, line, line_peer(d)).wait_recv()
            return carry

        lax.fori_loop(1, line_count, near_arrive, 0)
        each_hop(lambda direction, a=a: hop(a, direction).start(), True)

    for a in range(far_here):
        def far_whole(a=a):
            for t in range(3):
                far_own_in(t, a).wait()

            def far_arrive(d, carry):
                for t in range(3):
                    far_inward(t, a, me, peer(d)).wait_recv()
                return carry

            lax.fori_loop(1, count, far_arrive, 0)
            own_list(a, True).wait()

            def one(i):
                ids = [lists[near_here + a, i, e] for e in range(entries)]
                far_out[a][i] = attend_tile(ids, far_in[a][0, i], far_in[a], 1)

            def work(d, carry):
                one(peer(d))

                @pl.when(d > 1)
                def _():
                    far_outward(a, peer(d - 1), me).start()

                return carry

            lax.fori_loop(1, count, work, 0)
            one(me)
            far_outward(a, peer(count - 1), me).start()
            far_own_out(a).start()

        if_far(me, a, far_whole)

    for a in range(near_here):
        each_hop(lambda direction, a=a: hop(a, direction).wait_recv(), False)
        own_list(a, False).wait()

        def one(i, a=a):
            tile = blk * line_count + i
            first = (blk - 1) * line_count
            ids = [
                jnp.clip(lists[a, tile, e] - first, 0, 3 * line_count - 1) for e in range(entries)
            ]
            near_out[a][i] = attend_tile(ids, near_query[a][i], near_kv[a], 0)

        def work(d, carry, a=a, one=one):
            one(line_peer(d))

            @pl.when(d > 1)
            def _():
                near_outward(a, line_peer(d - 1), line).start()

            return carry

        lax.fori_loop(1, line_count, work, 0)
        one(line)
        near_outward(a, line_peer(line_count - 1), line).start()
        near_own_out(a).start()

    for a in range(far_here):
        def finish_own(a=a):
            far_own_out(a).wait()

            def sent_back(d, carry):
                far_outward(a, peer(d), me).wait_send()
                return carry

            lax.fori_loop(1, count, sent_back, 0)

        if_far(me, a, finish_own)

        def finish(d, carry, a=a):
            def other(d=d):
                for t in range(3):
                    far_inward(t, a, peer(d), me).wait_send()
                far_outward(a, me, peer(d)).wait_recv()

            if_far(peer(d), a, other)
            return carry

        lax.fori_loop(1, count, finish, 0)

    for a in range(near_here):
        near_own_out(a).wait()
        each_hop(lambda direction, a=a: hop(a, direction).wait_send(), True)

        def near_finish(d, carry, a=a):
            for t in range(3):
                near_inward(t, a, line_peer(d), line).wait_send()
            near_outward(a, line_peer(d), line).wait_send()
            near_outward(a, line, line_peer(d)).wait_recv()
            return carry

        lax.fori_loop(1, line_count, near_finish, 0)


def restore_kernel(place, landed, out_ref):
    for h in range(HEADS):
        out_ref[:, h * HEAD_DIM : (h + 1) * HEAD_DIM] = landed[place[h]]


def arrange_kernel(perm, q_ref, k_ref, v_ref, lists_ref, stage, list_rows):
    for slot in range(HEADS):
        columns = pl.ds(pl.multiple_of(perm[slot] * HEAD_DIM, HEAD_DIM), HEAD_DIM)
        for t, source in enumerate((q_ref, k_ref, v_ref)):
            stage[t, slot] = source[:, columns]
        list_rows[slot] = lists_ref[perm[slot]]


def arrange(perm, queries, keys, values, block_lists):
    rows, width = queries.shape
    steps = 4
    part = rows // steps
    block = pl.BlockSpec((part, width), lambda i: (i, 0))
    whole = pl.BlockSpec(block_lists.shape, lambda i: (0, 0, 0))
    return pl.pallas_call(
        arrange_kernel,
        grid=(steps,),
        out_shape=(
            jax.ShapeDtypeStruct((3, HEADS, rows, HEAD_DIM), jnp.bfloat16),
            jax.ShapeDtypeStruct(block_lists.shape, jnp.int32),
        ),
        in_specs=[pl.BlockSpec(memory_space=pltpu.SMEM), block, block, block, whole],
        out_specs=(pl.BlockSpec((3, HEADS, part, HEAD_DIM), lambda i: (0, 0, i, 0)), whole),
    )(perm, queries, keys, values, block_lists)


def whole_exchange(sizes, near, collective_id, stage, list_rows, place):
    line_count = sizes[1] * sizes[2]
    count = sizes[0] * line_count
    near_here = near // line_count
    far_here = -(-(HEADS - near) // count)
    rows = stage.shape[2]
    block = (rows, HEAD_DIM)
    anywhere = pl.BlockSpec(memory_space=pl.ANY)
    smem = pl.BlockSpec(memory_space=pltpu.SMEM)
    vmem = pl.BlockSpec(memory_space=pltpu.VMEM)
    dma = pltpu.SemaphoreType.DMA
    rows_here = near_here + far_here
    scratch = [pltpu.SMEM((rows_here,) + list_rows.shape[1:], jnp.int32), dma((rows_here,))]
    scratch += [pltpu.VMEM((3, count) + block, jnp.bfloat16)] * far_here
    scratch += [pltpu.VMEM((count,) + block, jnp.bfloat16)] * far_here
    scratch += [pltpu.VMEM((line_count,) + block, jnp.bfloat16)] * near_here
    scratch += [pltpu.VMEM((2, 3 * line_count) + block, jnp.bfloat16)] * near_here
    scratch += [pltpu.VMEM((line_count,) + block, jnp.bfloat16)] * near_here
    scratch += [dma((4, far_here, count))] * 2 + [dma((4, far_here))]
    if near:
        scratch += [dma((4, near_here, line_count))] * 2 + [dma((4, near_here))]
        scratch += [dma((near_here, 2))] * 2
    landed = pl.pallas_call(
        functools.partial(exchange_kernel, sizes, near),
        out_shape=jax.ShapeDtypeStruct((HEADS,) + block, jnp.bfloat16),
        in_specs=[anywhere, anywhere],
        out_specs=anywhere,
        scratch_shapes=scratch,
        compiler_params=pltpu.CompilerParams(
            collective_id=collective_id, has_side_effects=True
        ),
    )(stage, list_rows)
    return pl.pallas_call(
        restore_kernel,
        out_shape=jax.ShapeDtypeStruct((rows, HEADS * HEAD_DIM), jnp.bfloat16),
        in_specs=[smem, vmem],
        out_specs=vmem,
    )(place, landed)


def head_order(block_lists, line_count):
    heads, tiles, _ = block_lists.shape
    frame = jnp.arange(tiles, dtype=jnp.int32)[None, :, None] // line_count
    apart = jnp.abs(block_lists // line_count - frame)
    is_near = jnp.max(apart, axis=(1, 2)) <= 1
    ids = jnp.arange(heads, dtype=jnp.int32)
    ahead = jnp.where(
        is_near[:, None] == is_near[None, :],
        ids[None, :] < ids[:, None],
        is_near[None, :],
    )
    place = jnp.sum(ahead, axis=1, dtype=jnp.int32)
    perm = jnp.sum(jnp.where(place[None, :] == ids[:, None], ids[None, :], 0), axis=1)
    return perm.astype(jnp.int32), place, jnp.sum(is_near, dtype=jnp.int32)


def solution(mesh):
    sizes = tuple(mesh.shape[axis] for axis in ("blk", "head", "sub"))
    line_count = sizes[1] * sizes[2]
    count = sizes[0] * line_count

    def body(queries, keys, values, block_lists):
        if queries.shape[0] != TILE or HEADS % count or block_lists.shape[1] != count:
            return per_device(queries, keys, values, block_lists)
        perm, place, near_total = head_order(block_lists, line_count)
        nears = [n for n in NEAR_COUNTS if n % line_count == 0 and n < HEADS]
        choice = sum((near_total >= n).astype(jnp.int32) for n in nears[1:])
        stage, list_rows = arrange(perm, queries, keys, values, block_lists)
        branches = [
            functools.partial(whole_exchange, sizes, n, number)
            for number, n in enumerate(nears)
        ]
        return lax.switch(choice, branches, stage, list_rows, place)

    in_specs = (
        P(("grp", "blk", "head", "sub"), None),
        P(("grp", "blk", "head", "sub"), None),
        P(("grp", "blk", "head", "sub"), None),
        P(),
    )
    out_specs = P(("grp", "blk", "head", "sub"), None)
    return jax.shard_map(
        body, mesh=mesh, in_specs=in_specs, out_specs=out_specs, check_vma=False
    )
```

```python
import functools
import math

import jax
import jax.numpy as jnp
from jax import lax
from jax.experimental import pallas as pl
from jax.experimental.pallas import tpu as pltpu
from jax.sharding import PartitionSpec as P

HEADS = 32
HEAD_DIM = 128
TILE = 128


NEG_FLOOR = -1e30


def query_rows(block_lists, first_head, heads_here, query_tokens):
    tile_ids = jnp.arange(block_lists.shape[1], dtype=jnp.int32)
    lists_local = lax.dynamic_slice_in_dim(block_lists, first_head, heads_here, 0)
    tile_mask = jnp.any(lists_local[:, :, :, None] == tile_ids, axis=2).astype(jnp.bfloat16)
    query_onehot = ((query_tokens // TILE)[:, None] == tile_ids[None, :]).astype(jnp.bfloat16)
    listed = jnp.einsum("qi,hij->hqj", query_onehot, tile_mask, preferred_element_type=jnp.float32)
    return listed.astype(jnp.bfloat16)


def attend_block(state_now, key_block, value_block, allowed, query_local, score_scale):
    top_old, total_old, accum_old = state_now
    scores = (
        jnp.einsum("qhd,khd->hqk", query_local, key_block, preferred_element_type=jnp.float32)
        * score_scale
    )
    top_new = jnp.maximum(top_old, jnp.max(jnp.where(allowed, scores, NEG_FLOOR), axis=2))
    factor = jnp.exp(top_old - top_new)
    weights = jnp.where(allowed, jnp.exp(scores - top_new[:, :, None]), 0.0)
    total_new = total_old * factor + jnp.sum(weights, axis=2)
    product = jnp.einsum(
        "hqk,khd->qhd",
        weights.astype(jnp.bfloat16),
        value_block,
        preferred_element_type=jnp.float32,
    )
    accum_new = accum_old * jnp.transpose(factor)[:, :, None] + product
    return (top_new, total_new, accum_new)


def make_step(query_local, listed_rows, key_token, block_len, tile_total):
    score_scale = 1.0 / math.sqrt(HEAD_DIM)
    tile_ids = jnp.arange(tile_total, dtype=jnp.int32)

    def fold_step(state_now, piece, first_row):
        key_piece, value_piece = piece
        block_count = key_piece.shape[0] // block_len

        def one_block(block_index, state_in):
            key_block = lax.dynamic_slice_in_dim(key_piece, block_index * block_len, block_len, 0)
            value_block = lax.dynamic_slice_in_dim(
                value_piece, block_index * block_len, block_len, 0
            )
            positions = block_index * block_len + jnp.arange(block_len, dtype=jnp.int32)
            key_tiles = key_token(positions) // TILE
            key_onehot = (tile_ids[:, None] == key_tiles[None, :]).astype(jnp.bfloat16)
            allowed = (
                jnp.einsum(
                    "hqj,jk->hqk", listed_rows, key_onehot, preferred_element_type=jnp.float32
                )
                > 0.5
            )
            result = attend_block(
                state_in, key_block, value_block, allowed, query_local, score_scale
            )
            return result

        return lax.fori_loop(0, block_count, one_block, state_now)

    return fold_step


def start_state(heads_here, block_len):
    top_all = jnp.full((heads_here, block_len), NEG_FLOOR, jnp.float32)
    total_all = jnp.zeros((heads_here, block_len), jnp.float32)
    accum_all = jnp.zeros((block_len, heads_here, HEAD_DIM), jnp.float32)
    return (top_all, total_all, accum_all)


def normalize(state_end):
    top_all, total_all, accum_all = state_end
    return (accum_all / jnp.transpose(total_all)[:, :, None]).astype(jnp.bfloat16)


def per_device(queries, keys, values, block_lists):
    row_count, col_count = queries.shape
    n_head = lax.axis_size("head")
    n_sub = lax.axis_size("sub")
    blk_index = lax.axis_index("blk")
    head_index = lax.axis_index("head")
    sub_index = lax.axis_index("sub")
    tile_total = block_lists.shape[1]
    heads_here = HEADS // (n_head * n_sub)
    block_len = row_count * n_head * n_sub

    def inward(tensor):
        return tensor.reshape(1, 1, row_count, n_head, n_sub, heads_here * HEAD_DIM)

    query_six, keys_six, values_six = (
        lax.all_to_all(
            lax.all_to_all(inward(queries), "head", split_axis=3, concat_axis=1, tiled=True),
            "sub",
            split_axis=4,
            concat_axis=0,
            tiled=True,
        ),
        lax.all_to_all(
            lax.all_to_all(inward(keys), "head", split_axis=3, concat_axis=1, tiled=True),
            "sub",
            split_axis=4,
            concat_axis=0,
            tiled=True,
        ),
        lax.all_to_all(
            lax.all_to_all(inward(values), "head", split_axis=3, concat_axis=1, tiled=True),
            "sub",
            split_axis=4,
            concat_axis=0,
            tiled=True,
        ),
    )
    query_local = query_six.reshape(block_len, heads_here, HEAD_DIM)
    keys_local = keys_six.reshape(block_len, heads_here, HEAD_DIM)
    values_local = values_six.reshape(block_len, heads_here, HEAD_DIM)

    def key_token(positions):
        source_dev = positions // block_len
        within = positions % block_len
        sub_source = within // (n_head * row_count)
        head_source = within // row_count % n_head
        offset = within % row_count
        return ((source_dev * n_head + head_source) * n_sub + sub_source) * row_count + offset

    query_tokens = key_token(blk_index * block_len + jnp.arange(block_len, dtype=jnp.int32))
    first_head = (head_index * n_sub + sub_index) * heads_here
    listed_rows = query_rows(block_lists, first_head, heads_here, query_tokens)
    fold_step = make_step(query_local, listed_rows, key_token, block_len, tile_total)
    state_end = fold_step(
        start_state(heads_here, block_len),
        (
            lax.all_gather(keys_local, "blk", axis=0, tiled=True),
            lax.all_gather(values_local, "blk", axis=0, tiled=True),
        ),
        jnp.int32(0),
    )
    result_rows = normalize(state_end)
    attended = result_rows.reshape(n_sub, n_head, row_count, 1, 1, heads_here * HEAD_DIM)
    returned = lax.all_to_all(
        lax.all_to_all(attended, "head", split_axis=1, concat_axis=3, tiled=True),
        "sub",
        split_axis=0,
        concat_axis=4,
        tiled=True,
    )
    return returned.reshape(row_count, col_count)


NEAR_COUNTS = (0, 8, 12, 16, 20)


def attend_tile(ids, query, buf, first):
    score_scale = 1.0 / math.sqrt(HEAD_DIM)
    scores, top = [], None
    for tile in ids:
        s = lax.dot_general(
            query, buf[first, tile], (((1,), (1,)), ((), ())), preferred_element_type=jnp.float32
        ) * score_scale
        scores.append(s)
        top = s if top is None else jnp.maximum(top, s)
    row_top = jnp.max(top, axis=1, keepdims=True)
    total, accum = None, None
    for e, tile in enumerate(ids):
        w = jnp.exp(scores[e] - row_top)
        if e:
            repeat = tile == ids[0]
            for f in range(1, e):
                repeat = jnp.logical_or(repeat, tile == ids[f])
            w = w * jnp.where(repeat, 0.0, 1.0)
        part = jnp.dot(
            w.astype(jnp.bfloat16), buf[first + 1, tile], preferred_element_type=jnp.float32
        )
        total = w if total is None else total + w
        accum = part if accum is None else accum + part
    row_total = jnp.sum(total, axis=1, keepdims=True)
    return (accum / row_total).astype(jnp.bfloat16)


def exchange_kernel(sizes, entries, near, stage, list_rows, landed, lists, list_sem, *scratch):
    n_blk, n_head, n_sub = sizes
    line_count = n_head * n_sub
    count = n_blk * line_count
    near_here = near // line_count
    far = HEADS - near
    far_here = -(-far // count)
    far_in = scratch[:far_here]
    far_out = scratch[far_here : 2 * far_here]
    scratch = scratch[2 * far_here :]
    near_query = scratch[:near_here]
    near_kv = scratch[near_here : 2 * near_here]
    near_out = scratch[2 * near_here : 3 * near_here]
    far_send, far_recv, far_local = scratch[3 * near_here : 3 * near_here + 3]
    if near:
        near_send, near_recv, near_local, hop_send, hop_recv = scratch[3 * near_here + 3 :]

    blk = lax.axis_index("blk")
    line = lax.axis_index("head") * n_sub + lax.axis_index("sub")
    me = blk * line_count + line

    def remote(src, dst, send, recv, rank):
        return pltpu.make_async_remote_copy(
            src_ref=src,
            dst_ref=dst,
            send_sem=send,
            recv_sem=recv,
            device_id={
                "blk": rank // line_count,
                "head": rank // n_sub % n_head,
                "sub": rank % n_sub,
            },
            device_id_type=pl.DeviceIdType.MESH,
        )

    def peer(d):
        return (me + d) % count

    def line_peer(d):
        return (line + d) % line_count

    def far_number(rank, a):
        return a * count + rank // line_count + n_blk * (rank % line_count)

    def far_inward(t, a, target, sender):
        return remote(
            stage.at[t, near + far_number(target, a)], far_in[a].at[t, sender],
            far_send.at[t, a, target], far_recv.at[t, a, sender], target,
        )

    def far_outward(a, target, sender):
        return remote(
            far_out[a].at[target], landed.at[near + far_number(sender, a)],
            far_send.at[3, a, target], far_recv.at[3, a, sender], target,
        )

    def far_own_in(t, a):
        return pltpu.make_async_copy(
            stage.at[t, near + far_number(me, a)], far_in[a].at[t, me], far_local.at[t, a]
        )

    def far_own_out(a):
        return pltpu.make_async_copy(
            far_out[a].at[me], landed.at[near + far_number(me, a)], far_local.at[3, a]
        )

    def if_far(rank, a, action):
        if (a + 1) * count <= far:
            action()
        else:
            pl.when(far_number(rank, a) < far)(action)

    def near_slot(t, a, sender):
        if t == 0:
            return near_query[a].at[sender]
        return near_kv[a].at[t - 1, line_count + sender]

    def near_inward(t, a, target, sender):
        return remote(
            stage.at[t, a * line_count + target], near_slot(t, a, sender),
            near_send.at[t, a, target], near_recv.at[t, a, sender], blk * line_count + target,
        )

    def near_outward(a, target, sender):
        return remote(
            near_out[a].at[target], landed.at[a * line_count + sender],
            near_send.at[3, a, target], near_recv.at[3, a, sender], blk * line_count + target,
        )

    def near_own_in(t, a):
        return pltpu.make_async_copy(
            stage.at[t, a * line_count + line], near_slot(t, a, line), near_local.at[t, a]
        )

    def near_own_out(a):
        return pltpu.make_async_copy(
            near_out[a].at[line], landed.at[a * line_count + line], near_local.at[3, a]
        )

    def hop(a, direction):
        return remote(
            near_kv[a].at[:, pl.ds(line_count, line_count)],
            near_kv[a].at[:, pl.ds(2 * line_count * direction, line_count)],
            hop_send.at[a, direction], hop_recv.at[a, direction],
            (me + line_count if direction == 0 else me + count - line_count) % count,
        )

    def each_hop(action, sending):
        up, down = blk < n_blk - 1, blk > 0
        pl.when(up if sending else down)(functools.partial(action, 0))
        pl.when(down if sending else up)(functools.partial(action, 1))

    barrier = pltpu.get_barrier_semaphore()

    def greet(d, carry):
        rank = peer(d)
        pl.semaphore_signal(
            barrier, inc=1,
            device_id={
                "blk": rank // line_count,
                "head": rank // n_sub % n_head,
                "sub": rank % n_sub,
            },
            device_id_type=pl.DeviceIdType.MESH,
        )
        return carry

    lax.fori_loop(1, count, greet, 0)

    def own_list(a, far_head):
        slot = near + far_number(me, a) if far_head else a * line_count + line
        row = near_here + a if far_head else a
        return pltpu.make_async_copy(list_rows.at[slot], lists.at[row], list_sem.at[row])

    for a in range(near_here):
        own_list(a, False).start()
    for a in range(far_here):
        if_far(me, a, lambda a=a: own_list(a, True).start())
    pl.semaphore_wait(barrier, count - 1)

    for a in range(near_here):
        def near_send_in(d, carry, a=a):
            for t in (1, 2, 0):
                near_inward(t, a, line_peer(d), line).start()
            return carry

        lax.fori_loop(1, line_count, near_send_in, 0)
        for t in range(3):
            near_own_in(t, a).start()

    for a in range(far_here):
        def far_send_in(d, carry, a=a):
            def send(d=d):
                for t in range(3):
                    far_inward(t, a, peer(d), me).start()

            if_far(peer(d), a, send)
            return carry

        lax.fori_loop(1, count, far_send_in, 0)

        def own(a=a):
            for t in range(3):
                far_own_in(t, a).start()

        if_far(me, a, own)

    for a in range(near_here):
        for t in range(3):
            near_own_in(t, a).wait()

        def near_arrive(d, carry, a=a):
            for t in range(3):
                near_inward(t, a, line, line_peer(d)).wait_recv()
            return carry

        lax.fori_loop(1, line_count, near_arrive, 0)
        each_hop(lambda direction, a=a: hop(a, direction).start(), True)

    for a in range(far_here):
        def far_whole(a=a):
            for t in range(3):
                far_own_in(t, a).wait()

            def far_arrive(d, carry):
                for t in range(3):
                    far_inward(t, a, me, peer(d)).wait_recv()
                return carry

            lax.fori_loop(1, count, far_arrive, 0)
            own_list(a, True).wait()

            def one(i):
                ids = [lists[near_here + a, i * entries + e] for e in range(entries)]
                far_out[a][i] = attend_tile(ids, far_in[a][0, i], far_in[a], 1)

            def work(d, carry):
                one(peer(d))

                @pl.when(d > 1)
                def _():
                    far_outward(a, peer(d - 1), me).start()

                return carry

            lax.fori_loop(1, count, work, 0)
            one(me)
            far_outward(a, peer(count - 1), me).start()
            far_own_out(a).start()

        if_far(me, a, far_whole)

    for a in range(near_here):
        each_hop(lambda direction, a=a: hop(a, direction).wait_recv(), False)
        own_list(a, False).wait()

        def one(i, a=a):
            tile = blk * line_count + i
            first = (blk - 1) * line_count
            ids = [
                jnp.clip(lists[a, tile * entries + e] - first, 0, 3 * line_count - 1) for e in range(entries)
            ]
            near_out[a][i] = attend_tile(ids, near_query[a][i], near_kv[a], 0)

        def work(d, carry, a=a, one=one):
            one(line_peer(d))

            @pl.when(d > 1)
            def _():
                near_outward(a, line_peer(d - 1), line).start()

            return carry

        lax.fori_loop(1, line_count, work, 0)
        one(line)
        near_outward(a, line_peer(line_count - 1), line).start()
        near_own_out(a).start()

    for a in range(far_here):
        def finish_own(a=a):
            far_own_out(a).wait()

            def sent_back(d, carry):
                far_outward(a, peer(d), me).wait_send()
                return carry

            lax.fori_loop(1, count, sent_back, 0)

        if_far(me, a, finish_own)

        def finish(d, carry, a=a):
            def other(d=d):
                for t in range(3):
                    far_inward(t, a, peer(d), me).wait_send()
                far_outward(a, me, peer(d)).wait_recv()

            if_far(peer(d), a, other)
            return carry

        lax.fori_loop(1, count, finish, 0)

    for a in range(near_here):
        near_own_out(a).wait()
        each_hop(lambda direction, a=a: hop(a, direction).wait_send(), True)

        def near_finish(d, carry, a=a):
            for t in range(3):
                near_inward(t, a, line_peer(d), line).wait_send()
            near_outward(a, line_peer(d), line).wait_send()
            near_outward(a, line, line_peer(d)).wait_recv()
            return carry

        lax.fori_loop(1, line_count, near_finish, 0)


def restore_kernel(place, landed, out_ref):
    for h in range(HEADS):
        out_ref[:, h * HEAD_DIM : (h + 1) * HEAD_DIM] = landed[place[h]]


def arrange_kernel(frames, line_count, nears, lists_ref, q_ref, k_ref, v_ref, stage, list_rows,
                   place_out, choice_out, order, order_scalar, order_sem):
    @pl.when(pl.program_id(0) == 0)
    def _():
        ids = lists_ref[...]
        steps, heads = ids.shape
        per_frame = steps // frames
        away = None
        for f in range(frames):
            part = ids[f * per_frame : (f + 1) * per_frame]
            outside = jnp.logical_or(
                part < (f - 1) * line_count, part >= (f + 2) * line_count
            )
            found = jnp.max(jnp.where(outside, 1, 0), axis=0, keepdims=True)
            away = found if away is None else jnp.maximum(away, found)
        row = lax.broadcasted_iota(jnp.int32, (heads, heads), 0)
        col = lax.broadcasted_iota(jnp.int32, (heads, heads), 1)
        away_col = jnp.broadcast_to(away, (heads, heads))
        away_row = jnp.broadcast_to(
            jnp.sum(jnp.where(row == col, away_col, 0), axis=1, keepdims=True), (heads, heads)
        )
        same = away_row == away_col
        ahead = jnp.where(same, jnp.where(row < col, 1, 0), away_col)
        place = jnp.sum(ahead, axis=0, keepdims=True)
        picks = jnp.broadcast_to(place, (heads, heads)) == row
        behind = jnp.where(same, jnp.where(col < row, 1, 0), away_row)
        place_of_row = jnp.sum(behind, axis=1, keepdims=True)
        perm = jnp.sum(
            jnp.where(jnp.broadcast_to(place_of_row, (heads, heads)) == col, row, 0),
            axis=0, keepdims=True,
        )
        near_total = heads - jnp.sum(away, axis=1, keepdims=True)
        choice = jnp.zeros((1, 1), jnp.int32)
        for n in nears[1:]:
            choice = choice + jnp.where(near_total >= n, 1, 0)
        order[0:1, 0:heads] = perm
        order[1:2, 0:heads] = place
        order[2:3, 0:heads] = jnp.broadcast_to(choice, (1, heads))
        copy = pltpu.make_async_copy(order, order_scalar, order_sem)
        copy.start()
        rows_now = lax.dot_general(
            jnp.where(picks, 1.0, 0.0).astype(jnp.bfloat16),
            ids.astype(jnp.float32).astype(jnp.bfloat16),
            (((1,), (1,)), ((), ())),
            preferred_element_type=jnp.float32,
        )
        list_rows[...] = rows_now.astype(jnp.int32)
        copy.wait()
        for h in range(heads):
            place_out[h] = order_scalar[1, h]
        choice_out[0] = order_scalar[2, 0]

    for slot in range(HEADS):
        columns = pl.ds(pl.multiple_of(order_scalar[0, slot] * HEAD_DIM, HEAD_DIM), HEAD_DIM)
        for t, source in enumerate((q_ref, k_ref, v_ref)):
            stage[t, slot] = source[:, columns]


def arrange(line_count, nears, queries, keys, values, block_lists):
    rows, width = queries.shape
    heads, tiles, entries = block_lists.shape
    steps = 4
    part = rows // steps
    block = pl.BlockSpec((part, width), lambda i: (i, 0))
    by_row = jnp.transpose(block_lists, (1, 2, 0)).reshape(tiles * entries, heads)
    smem = pl.BlockSpec(memory_space=pltpu.SMEM)
    return pl.pallas_call(
        functools.partial(arrange_kernel, tiles // line_count, line_count, nears),
        grid=(steps,),
        out_shape=(
            jax.ShapeDtypeStruct((3, HEADS, rows, HEAD_DIM), jnp.bfloat16),
            jax.ShapeDtypeStruct((heads, tiles * entries), jnp.int32),
            jax.ShapeDtypeStruct((heads,), jnp.int32),
            jax.ShapeDtypeStruct((1,), jnp.int32),
        ),
        in_specs=[pl.BlockSpec(by_row.shape, lambda i: (0, 0)), block, block, block],
        out_specs=(
            pl.BlockSpec((3, HEADS, part, HEAD_DIM), lambda i: (0, 0, i, 0)),
            pl.BlockSpec((heads, tiles * entries), lambda i: (0, 0)),
            smem,
            smem,
        ),
        scratch_shapes=[
            pltpu.VMEM((8, 128), jnp.int32),
            pltpu.SMEM((8, 128), jnp.int32),
            pltpu.SemaphoreType.DMA,
        ],
    )(by_row, queries, keys, values)


def whole_exchange(sizes, entries, near, collective_id, stage, list_rows, place):
    line_count = sizes[1] * sizes[2]
    count = sizes[0] * line_count
    near_here = near // line_count
    far_here = -(-(HEADS - near) // count)
    rows = stage.shape[2]
    block = (rows, HEAD_DIM)
    anywhere = pl.BlockSpec(memory_space=pl.ANY)
    smem = pl.BlockSpec(memory_space=pltpu.SMEM)
    vmem = pl.BlockSpec(memory_space=pltpu.VMEM)
    dma = pltpu.SemaphoreType.DMA
    rows_here = near_here + far_here
    scratch = [pltpu.SMEM((rows_here,) + list_rows.shape[1:], jnp.int32), dma((rows_here,))]
    scratch += [pltpu.VMEM((3, count) + block, jnp.bfloat16)] * far_here
    scratch += [pltpu.VMEM((count,) + block, jnp.bfloat16)] * far_here
    scratch += [pltpu.VMEM((line_count,) + block, jnp.bfloat16)] * near_here
    scratch += [pltpu.VMEM((2, 3 * line_count) + block, jnp.bfloat16)] * near_here
    scratch += [pltpu.VMEM((line_count,) + block, jnp.bfloat16)] * near_here
    scratch += [dma((4, far_here, count))] * 2 + [dma((4, far_here))]
    if near:
        scratch += [dma((4, near_here, line_count))] * 2 + [dma((4, near_here))]
        scratch += [dma((near_here, 2))] * 2
    landed = pl.pallas_call(
        functools.partial(exchange_kernel, sizes, entries, near),
        out_shape=jax.ShapeDtypeStruct((HEADS,) + block, jnp.bfloat16),
        in_specs=[anywhere, anywhere],
        out_specs=anywhere,
        scratch_shapes=scratch,
        compiler_params=pltpu.CompilerParams(
            collective_id=collective_id, has_side_effects=True
        ),
    )(stage, list_rows)
    return pl.pallas_call(
        restore_kernel,
        out_shape=jax.ShapeDtypeStruct((rows, HEADS * HEAD_DIM), jnp.bfloat16),
        in_specs=[smem, vmem],
        out_specs=vmem,
    )(place, landed)


def solution(mesh):
    sizes = tuple(mesh.shape[axis] for axis in ("blk", "head", "sub"))
    line_count = sizes[1] * sizes[2]
    count = sizes[0] * line_count

    def body(queries, keys, values, block_lists):
        if queries.shape[0] != TILE or HEADS % count or block_lists.shape[1] != count:
            return per_device(queries, keys, values, block_lists)
        nears = [n for n in NEAR_COUNTS if n % line_count == 0 and n < HEADS]
        stage, list_rows, place, choice = arrange(
            line_count, nears, queries, keys, values, block_lists
        )
        branches = [
            functools.partial(whole_exchange, sizes, block_lists.shape[2], n, number)
            for number, n in enumerate(nears)
        ]
        return lax.switch(choice[0], branches, stage, list_rows, place)

    in_specs = (
        P(("grp", "blk", "head", "sub"), None),
        P(("grp", "blk", "head", "sub"), None),
        P(("grp", "blk", "head", "sub"), None),
        P(),
    )
    out_specs = P(("grp", "blk", "head", "sub"), None)
    return jax.shard_map(
        body, mesh=mesh, in_specs=in_specs, out_specs=out_specs, check_vma=False
    )
```

```python
import functools
import math

import jax
import jax.numpy as jnp
from jax import lax
from jax.experimental import pallas as pl
from jax.experimental.pallas import tpu as pltpu
from jax.sharding import PartitionSpec as P

HEADS = 32
HEAD_DIM = 128
TILE = 128


NEG_FLOOR = -1e30


def query_rows(block_lists, first_head, heads_here, query_tokens):
    tile_ids = jnp.arange(block_lists.shape[1], dtype=jnp.int32)
    lists_local = lax.dynamic_slice_in_dim(block_lists, first_head, heads_here, 0)
    tile_mask = jnp.any(lists_local[:, :, :, None] == tile_ids, axis=2).astype(jnp.bfloat16)
    query_onehot = ((query_tokens // TILE)[:, None] == tile_ids[None, :]).astype(jnp.bfloat16)
    listed = jnp.einsum("qi,hij->hqj", query_onehot, tile_mask, preferred_element_type=jnp.float32)
    return listed.astype(jnp.bfloat16)


def attend_block(state_now, key_block, value_block, allowed, query_local, score_scale):
    top_old, total_old, accum_old = state_now
    scores = (
        jnp.einsum("qhd,khd->hqk", query_local, key_block, preferred_element_type=jnp.float32)
        * score_scale
    )
    top_new = jnp.maximum(top_old, jnp.max(jnp.where(allowed, scores, NEG_FLOOR), axis=2))
    factor = jnp.exp(top_old - top_new)
    weights = jnp.where(allowed, jnp.exp(scores - top_new[:, :, None]), 0.0)
    total_new = total_old * factor + jnp.sum(weights, axis=2)
    product = jnp.einsum(
        "hqk,khd->qhd",
        weights.astype(jnp.bfloat16),
        value_block,
        preferred_element_type=jnp.float32,
    )
    accum_new = accum_old * jnp.transpose(factor)[:, :, None] + product
    return (top_new, total_new, accum_new)


def make_step(query_local, listed_rows, key_token, block_len, tile_total):
    score_scale = 1.0 / math.sqrt(HEAD_DIM)
    tile_ids = jnp.arange(tile_total, dtype=jnp.int32)

    def fold_step(state_now, piece, first_row):
        key_piece, value_piece = piece
        block_count = key_piece.shape[0] // block_len

        def one_block(block_index, state_in):
            key_block = lax.dynamic_slice_in_dim(key_piece, block_index * block_len, block_len, 0)
            value_block = lax.dynamic_slice_in_dim(
                value_piece, block_index * block_len, block_len, 0
            )
            positions = block_index * block_len + jnp.arange(block_len, dtype=jnp.int32)
            key_tiles = key_token(positions) // TILE
            key_onehot = (tile_ids[:, None] == key_tiles[None, :]).astype(jnp.bfloat16)
            allowed = (
                jnp.einsum(
                    "hqj,jk->hqk", listed_rows, key_onehot, preferred_element_type=jnp.float32
                )
                > 0.5
            )
            result = attend_block(
                state_in, key_block, value_block, allowed, query_local, score_scale
            )
            return result

        return lax.fori_loop(0, block_count, one_block, state_now)

    return fold_step


def start_state(heads_here, block_len):
    top_all = jnp.full((heads_here, block_len), NEG_FLOOR, jnp.float32)
    total_all = jnp.zeros((heads_here, block_len), jnp.float32)
    accum_all = jnp.zeros((block_len, heads_here, HEAD_DIM), jnp.float32)
    return (top_all, total_all, accum_all)


def normalize(state_end):
    top_all, total_all, accum_all = state_end
    return (accum_all / jnp.transpose(total_all)[:, :, None]).astype(jnp.bfloat16)


def per_device(queries, keys, values, block_lists):
    row_count, col_count = queries.shape
    n_head = lax.axis_size("head")
    n_sub = lax.axis_size("sub")
    blk_index = lax.axis_index("blk")
    head_index = lax.axis_index("head")
    sub_index = lax.axis_index("sub")
    tile_total = block_lists.shape[1]
    heads_here = HEADS // (n_head * n_sub)
    block_len = row_count * n_head * n_sub

    def inward(tensor):
        return tensor.reshape(1, 1, row_count, n_head, n_sub, heads_here * HEAD_DIM)

    query_six, keys_six, values_six = (
        lax.all_to_all(
            lax.all_to_all(inward(queries), "head", split_axis=3, concat_axis=1, tiled=True),
            "sub",
            split_axis=4,
            concat_axis=0,
            tiled=True,
        ),
        lax.all_to_all(
            lax.all_to_all(inward(keys), "head", split_axis=3, concat_axis=1, tiled=True),
            "sub",
            split_axis=4,
            concat_axis=0,
            tiled=True,
        ),
        lax.all_to_all(
            lax.all_to_all(inward(values), "head", split_axis=3, concat_axis=1, tiled=True),
            "sub",
            split_axis=4,
            concat_axis=0,
            tiled=True,
        ),
    )
    query_local = query_six.reshape(block_len, heads_here, HEAD_DIM)
    keys_local = keys_six.reshape(block_len, heads_here, HEAD_DIM)
    values_local = values_six.reshape(block_len, heads_here, HEAD_DIM)

    def key_token(positions):
        source_dev = positions // block_len
        within = positions % block_len
        sub_source = within // (n_head * row_count)
        head_source = within // row_count % n_head
        offset = within % row_count
        return ((source_dev * n_head + head_source) * n_sub + sub_source) * row_count + offset

    query_tokens = key_token(blk_index * block_len + jnp.arange(block_len, dtype=jnp.int32))
    first_head = (head_index * n_sub + sub_index) * heads_here
    listed_rows = query_rows(block_lists, first_head, heads_here, query_tokens)
    fold_step = make_step(query_local, listed_rows, key_token, block_len, tile_total)
    state_end = fold_step(
        start_state(heads_here, block_len),
        (
            lax.all_gather(keys_local, "blk", axis=0, tiled=True),
            lax.all_gather(values_local, "blk", axis=0, tiled=True),
        ),
        jnp.int32(0),
    )
    result_rows = normalize(state_end)
    attended = result_rows.reshape(n_sub, n_head, row_count, 1, 1, heads_here * HEAD_DIM)
    returned = lax.all_to_all(
        lax.all_to_all(attended, "head", split_axis=1, concat_axis=3, tiled=True),
        "sub",
        split_axis=0,
        concat_axis=4,
        tiled=True,
    )
    return returned.reshape(row_count, col_count)


NEAR_COUNTS = (0, 8, 12, 16, 20)


def attend_tile(ids, query, buf, first):
    score_scale = 1.0 / math.sqrt(HEAD_DIM)
    scores, top = [], None
    for tile in ids:
        s = lax.dot_general(
            query, buf[first, tile], (((1,), (1,)), ((), ())), preferred_element_type=jnp.float32
        ) * score_scale
        scores.append(s)
        top = s if top is None else jnp.maximum(top, s)
    row_top = jnp.max(top, axis=1, keepdims=True)
    total, accum = None, None
    for e, tile in enumerate(ids):
        w = jnp.exp(scores[e] - row_top)
        if e:
            repeat = tile == ids[0]
            for f in range(1, e):
                repeat = jnp.logical_or(repeat, tile == ids[f])
            w = w * jnp.where(repeat, 0.0, 1.0)
        part = jnp.dot(
            w.astype(jnp.bfloat16), buf[first + 1, tile], preferred_element_type=jnp.float32
        )
        total = w if total is None else total + w
        accum = part if accum is None else accum + part
    row_total = jnp.sum(total, axis=1, keepdims=True)
    return (accum / row_total).astype(jnp.bfloat16)


def exchange_kernel(sizes, entries, near, stage, list_rows, landed, lists, list_sem, *scratch):
    n_blk, n_head, n_sub = sizes
    line_count = n_head * n_sub
    count = n_blk * line_count
    near_here = near // line_count
    far = HEADS - near
    far_here = -(-far // count)
    far_in = scratch[:far_here]
    far_out = scratch[far_here : 2 * far_here]
    scratch = scratch[2 * far_here :]
    near_query = scratch[:near_here]
    near_kv = scratch[near_here : 2 * near_here]
    near_out = scratch[2 * near_here : 3 * near_here]
    far_send, far_recv, far_local = scratch[3 * near_here : 3 * near_here + 3]
    if near:
        near_send, near_recv, near_local, hop_send, hop_recv = scratch[3 * near_here + 3 :]

    blk = lax.axis_index("blk")
    line = lax.axis_index("head") * n_sub + lax.axis_index("sub")
    me = blk * line_count + line

    def remote(src, dst, send, recv, rank):
        return pltpu.make_async_remote_copy(
            src_ref=src,
            dst_ref=dst,
            send_sem=send,
            recv_sem=recv,
            device_id={
                "blk": rank // line_count,
                "head": rank // n_sub % n_head,
                "sub": rank % n_sub,
            },
            device_id_type=pl.DeviceIdType.MESH,
        )

    def peer(d):
        return (me + d) % count

    def line_peer(d):
        return (line + d) % line_count

    def far_number(rank, a):
        turn = (rank % line_count + count - rank // line_count) % line_count
        return a * count + rank // line_count + n_blk * turn

    def far_inward(t, a, target, sender):
        return remote(
            stage.at[t, near + far_number(target, a)], far_in[a].at[t, sender],
            far_send.at[t, a, target], far_recv.at[t, a, sender], target,
        )

    def far_outward(a, target, sender):
        return remote(
            far_out[a].at[target], landed.at[near + far_number(sender, a)],
            far_send.at[3, a, target], far_recv.at[3, a, sender], target,
        )

    def far_own_in(t, a):
        return pltpu.make_async_copy(
            stage.at[t, near + far_number(me, a)], far_in[a].at[t, me], far_local.at[t, a]
        )

    def far_own_out(a):
        return pltpu.make_async_copy(
            far_out[a].at[me], landed.at[near + far_number(me, a)], far_local.at[3, a]
        )

    def if_far(rank, a, action):
        if (a + 1) * count <= far:
            action()
        else:
            pl.when(far_number(rank, a) < far)(action)

    def near_slot(t, a, sender):
        if t == 0:
            return near_query[a].at[sender]
        return near_kv[a].at[t - 1, line_count + sender]

    def near_inward(t, a, target, sender):
        return remote(
            stage.at[t, a * line_count + target], near_slot(t, a, sender),
            near_send.at[t, a, target], near_recv.at[t, a, sender], blk * line_count + target,
        )

    def near_outward(a, target, sender):
        return remote(
            near_out[a].at[target], landed.at[a * line_count + sender],
            near_send.at[3, a, target], near_recv.at[3, a, sender], blk * line_count + target,
        )

    def near_own_in(t, a):
        return pltpu.make_async_copy(
            stage.at[t, a * line_count + line], near_slot(t, a, line), near_local.at[t, a]
        )

    def near_own_out(a):
        return pltpu.make_async_copy(
            near_out[a].at[line], landed.at[a * line_count + line], near_local.at[3, a]
        )

    def hop(a, direction):
        return remote(
            near_kv[a].at[:, pl.ds(line_count, line_count)],
            near_kv[a].at[:, pl.ds(2 * line_count * direction, line_count)],
            hop_send.at[a, direction], hop_recv.at[a, direction],
            (me + line_count if direction == 0 else me + count - line_count) % count,
        )

    def each_hop(action, sending):
        up, down = blk < n_blk - 1, blk > 0
        pl.when(up if sending else down)(functools.partial(action, 0))
        pl.when(down if sending else up)(functools.partial(action, 1))

    barrier = pltpu.get_barrier_semaphore()

    def greet(d, carry):
        rank = peer(d)
        pl.semaphore_signal(
            barrier, inc=1,
            device_id={
                "blk": rank // line_count,
                "head": rank // n_sub % n_head,
                "sub": rank % n_sub,
            },
            device_id_type=pl.DeviceIdType.MESH,
        )
        return carry

    lax.fori_loop(1, count, greet, 0)

    def own_list(a, far_head):
        slot = near + far_number(me, a) if far_head else a * line_count + line
        row = near_here + a if far_head else a
        return pltpu.make_async_copy(list_rows.at[slot], lists.at[row], list_sem.at[row])

    for a in range(near_here):
        own_list(a, False).start()
    for a in range(far_here):
        if_far(me, a, lambda a=a: own_list(a, True).start())
    pl.semaphore_wait(barrier, count - 1)

    for a in range(near_here):
        def near_send_in(d, carry, a=a):
            for t in (1, 2, 0):
                near_inward(t, a, line_peer(d), line).start()
            return carry

        lax.fori_loop(1, line_count, near_send_in, 0)
        for t in range(3):
            near_own_in(t, a).start()

    for a in range(far_here):
        def far_send_in(d, carry, a=a):
            def send(d=d):
                for t in range(3):
                    far_inward(t, a, peer(d), me).start()

            if_far(peer(d), a, send)
            return carry

        lax.fori_loop(1, count, far_send_in, 0)

        def own(a=a):
            for t in range(3):
                far_own_in(t, a).start()

        if_far(me, a, own)

    for a in range(near_here):
        for t in range(3):
            near_own_in(t, a).wait()

        def near_arrive(d, carry, a=a):
            for t in range(3):
                near_inward(t, a, line, line_peer(d)).wait_recv()
            return carry

        lax.fori_loop(1, line_count, near_arrive, 0)
        each_hop(lambda direction, a=a: hop(a, direction).start(), True)

    for a in range(far_here):
        def far_whole(a=a):
            for t in range(3):
                far_own_in(t, a).wait()

            def far_arrive(d, carry):
                for t in range(3):
                    far_inward(t, a, me, peer(d)).wait_recv()
                return carry

            lax.fori_loop(1, count, far_arrive, 0)
            own_list(a, True).wait()

            def one(i):
                ids = [lists[near_here + a, i * entries + e] for e in range(entries)]
                far_out[a][i] = attend_tile(ids, far_in[a][0, i], far_in[a], 1)

            def work(d, carry):
                one(peer(d))

                @pl.when(d > 1)
                def _():
                    far_outward(a, peer(d - 1), me).start()

                return carry

            lax.fori_loop(1, count, work, 0)
            one(me)
            far_outward(a, peer(count - 1), me).start()
            far_own_out(a).start()

        if_far(me, a, far_whole)

    for a in range(near_here):
        each_hop(lambda direction, a=a: hop(a, direction).wait_recv(), False)
        own_list(a, False).wait()

        def one(i, a=a):
            tile = blk * line_count + i
            first = (blk - 1) * line_count
            ids = [
                jnp.clip(lists[a, tile * entries + e] - first, 0, 3 * line_count - 1) for e in range(entries)
            ]
            near_out[a][i] = attend_tile(ids, near_query[a][i], near_kv[a], 0)

        def work(d, carry, a=a, one=one):
            one(line_peer(d))

            @pl.when(d > 1)
            def _():
                near_outward(a, line_peer(d - 1), line).start()

            return carry

        lax.fori_loop(1, line_count, work, 0)
        one(line)
        near_outward(a, line_peer(line_count - 1), line).start()
        near_own_out(a).start()

    for a in range(far_here):
        def finish_own(a=a):
            far_own_out(a).wait()

            def sent_back(d, carry):
                far_outward(a, peer(d), me).wait_send()
                return carry

            lax.fori_loop(1, count, sent_back, 0)

        if_far(me, a, finish_own)

        def finish(d, carry, a=a):
            def other(d=d):
                for t in range(3):
                    far_inward(t, a, peer(d), me).wait_send()
                far_outward(a, me, peer(d)).wait_recv()

            if_far(peer(d), a, other)
            return carry

        lax.fori_loop(1, count, finish, 0)

    for a in range(near_here):
        near_own_out(a).wait()
        each_hop(lambda direction, a=a: hop(a, direction).wait_send(), True)

        def near_finish(d, carry, a=a):
            for t in range(3):
                near_inward(t, a, line_peer(d), line).wait_send()
            near_outward(a, line_peer(d), line).wait_send()
            near_outward(a, line, line_peer(d)).wait_recv()
            return carry

        lax.fori_loop(1, line_count, near_finish, 0)


def restore_kernel(place, landed, out_ref):
    for h in range(HEADS):
        out_ref[:, h * HEAD_DIM : (h + 1) * HEAD_DIM] = landed[place[h]]


def arrange_kernel(frames, line_count, nears, lists_ref, q_ref, k_ref, v_ref, stage, list_rows,
                   place_out, choice_out, order, order_scalar, order_sem):
    @pl.when(pl.program_id(0) == 0)
    def _():
        ids = lists_ref[...]
        steps, heads = ids.shape
        per_frame = steps // frames
        away = None
        for f in range(frames):
            part = ids[f * per_frame : (f + 1) * per_frame]
            outside = jnp.logical_or(
                part < (f - 1) * line_count, part >= (f + 2) * line_count
            )
            found = jnp.max(jnp.where(outside, 1, 0), axis=0, keepdims=True)
            away = found if away is None else jnp.maximum(away, found)
        row = lax.broadcasted_iota(jnp.int32, (heads, heads), 0)
        col = lax.broadcasted_iota(jnp.int32, (heads, heads), 1)
        away_col = jnp.broadcast_to(away, (heads, heads))
        away_row = jnp.broadcast_to(
            jnp.sum(jnp.where(row == col, away_col, 0), axis=1, keepdims=True), (heads, heads)
        )
        same = away_row == away_col
        ahead = jnp.where(same, jnp.where(row < col, 1, 0), away_col)
        place = jnp.sum(ahead, axis=0, keepdims=True)
        picks = jnp.broadcast_to(place, (heads, heads)) == row
        behind = jnp.where(same, jnp.where(col < row, 1, 0), away_row)
        place_of_row = jnp.sum(behind, axis=1, keepdims=True)
        perm = jnp.sum(
            jnp.where(jnp.broadcast_to(place_of_row, (heads, heads)) == col, row, 0),
            axis=0, keepdims=True,
        )
        near_total = heads - jnp.sum(away, axis=1, keepdims=True)
        choice = jnp.zeros((1, 1), jnp.int32)
        for n in nears[1:]:
            choice = choice + jnp.where(near_total >= n, 1, 0)
        order[0:1, 0:heads] = perm
        order[1:2, 0:heads] = place
        order[2:3, 0:heads] = jnp.broadcast_to(choice, (1, heads))
        copy = pltpu.make_async_copy(order, order_scalar, order_sem)
        copy.start()
        rows_now = lax.dot_general(
            jnp.where(picks, 1.0, 0.0).astype(jnp.bfloat16),
            ids.astype(jnp.float32).astype(jnp.bfloat16),
            (((1,), (1,)), ((), ())),
            preferred_element_type=jnp.float32,
        )
        list_rows[...] = rows_now.astype(jnp.int32)
        copy.wait()
        for h in range(heads):
            place_out[h] = order_scalar[1, h]
        choice_out[0] = order_scalar[2, 0]

    for slot in range(HEADS):
        columns = pl.ds(pl.multiple_of(order_scalar[0, slot] * HEAD_DIM, HEAD_DIM), HEAD_DIM)
        for t, source in enumerate((q_ref, k_ref, v_ref)):
            stage[t, slot] = source[:, columns]


def arrange(line_count, nears, queries, keys, values, block_lists):
    rows, width = queries.shape
    heads, tiles, entries = block_lists.shape
    steps = 4
    part = rows // steps
    block = pl.BlockSpec((part, width), lambda i: (i, 0))
    by_row = jnp.transpose(block_lists, (1, 2, 0)).reshape(tiles * entries, heads)
    smem = pl.BlockSpec(memory_space=pltpu.SMEM)
    return pl.pallas_call(
        functools.partial(arrange_kernel, tiles // line_count, line_count, nears),
        grid=(steps,),
        out_shape=(
            jax.ShapeDtypeStruct((3, HEADS, rows, HEAD_DIM), jnp.bfloat16),
            jax.ShapeDtypeStruct((heads, tiles * entries), jnp.int32),
            jax.ShapeDtypeStruct((heads,), jnp.int32),
            jax.ShapeDtypeStruct((1,), jnp.int32),
        ),
        in_specs=[pl.BlockSpec(by_row.shape, lambda i: (0, 0)), block, block, block],
        out_specs=(
            pl.BlockSpec((3, HEADS, part, HEAD_DIM), lambda i: (0, 0, i, 0)),
            pl.BlockSpec((heads, tiles * entries), lambda i: (0, 0)),
            smem,
            smem,
        ),
        scratch_shapes=[
            pltpu.VMEM((8, 128), jnp.int32),
            pltpu.SMEM((8, 128), jnp.int32),
            pltpu.SemaphoreType.DMA,
        ],
    )(by_row, queries, keys, values)


def whole_exchange(sizes, entries, near, collective_id, stage, list_rows, place):
    line_count = sizes[1] * sizes[2]
    count = sizes[0] * line_count
    near_here = near // line_count
    far_here = -(-(HEADS - near) // count)
    rows = stage.shape[2]
    block = (rows, HEAD_DIM)
    anywhere = pl.BlockSpec(memory_space=pl.ANY)
    smem = pl.BlockSpec(memory_space=pltpu.SMEM)
    vmem = pl.BlockSpec(memory_space=pltpu.VMEM)
    dma = pltpu.SemaphoreType.DMA
    rows_here = near_here + far_here
    scratch = [pltpu.SMEM((rows_here,) + list_rows.shape[1:], jnp.int32), dma((rows_here,))]
    scratch += [pltpu.VMEM((3, count) + block, jnp.bfloat16)] * far_here
    scratch += [pltpu.VMEM((count,) + block, jnp.bfloat16)] * far_here
    scratch += [pltpu.VMEM((line_count,) + block, jnp.bfloat16)] * near_here
    scratch += [pltpu.VMEM((2, 3 * line_count) + block, jnp.bfloat16)] * near_here
    scratch += [pltpu.VMEM((line_count,) + block, jnp.bfloat16)] * near_here
    scratch += [dma((4, far_here, count))] * 2 + [dma((4, far_here))]
    if near:
        scratch += [dma((4, near_here, line_count))] * 2 + [dma((4, near_here))]
        scratch += [dma((near_here, 2))] * 2
    landed = pl.pallas_call(
        functools.partial(exchange_kernel, sizes, entries, near),
        out_shape=jax.ShapeDtypeStruct((HEADS,) + block, jnp.bfloat16),
        in_specs=[anywhere, anywhere],
        out_specs=anywhere,
        scratch_shapes=scratch,
        compiler_params=pltpu.CompilerParams(
            collective_id=collective_id, has_side_effects=True
        ),
    )(stage, list_rows)
    return pl.pallas_call(
        restore_kernel,
        out_shape=jax.ShapeDtypeStruct((rows, HEADS * HEAD_DIM), jnp.bfloat16),
        in_specs=[smem, vmem],
        out_specs=vmem,
    )(place, landed)


def solution(mesh):
    sizes = tuple(mesh.shape[axis] for axis in ("blk", "head", "sub"))
    line_count = sizes[1] * sizes[2]
    count = sizes[0] * line_count

    def body(queries, keys, values, block_lists):
        if queries.shape[0] != TILE or HEADS % count or block_lists.shape[1] != count:
            return per_device(queries, keys, values, block_lists)
        nears = [n for n in NEAR_COUNTS if n % line_count == 0 and n < HEADS]
        stage, list_rows, place, choice = arrange(
            line_count, nears, queries, keys, values, block_lists
        )
        branches = [
            functools.partial(whole_exchange, sizes, block_lists.shape[2], n, number)
            for number, n in enumerate(nears)
        ]
        return lax.switch(choice[0], branches, stage, list_rows, place)

    in_specs = (
        P(("grp", "blk", "head", "sub"), None),
        P(("grp", "blk", "head", "sub"), None),
        P(("grp", "blk", "head", "sub"), None),
        P(),
    )
    out_specs = P(("grp", "blk", "head", "sub"), None)
    return jax.shard_map(
        body, mesh=mesh, in_specs=in_specs, out_specs=out_specs, check_vma=False
    )
```
